32 devices in a mesh: dp: 2 (over x), pipe: 4 (over z), mp: 4 (over y, core).
Axes of the slice: x: 2, y: 2, z: 4, core: 2. Of those that a mesh axis runs over, the one named last changes fastest.
Arguments:
- inputs: bfloat16 [4, 128, 1024], P(None, 'dp', 'mp'), may hold values from -6 to 6
- cotangent: bfloat16 [4, 128, 1024], P(None, 'dp', 'mp'), may hold values from -6 to 6
- gain: float32 [4, 1024], P('pipe'), may hold values from 0.25 to 1.75
- weight_in: bfloat16 [4, 1024, 32768], P('pipe', None, 'mp'), may hold values from -0.1875 to 0.1875
- weight_out: bfloat16 [4, 32768, 1024], P('pipe', 'mp'), may hold values from -0.03125 to 0.03125
Outputs:
- grad_in: bfloat16 [4, 1024, 32768], P('pipe', 'dp', 'mp')
- grad_out: bfloat16 [4, 32768, 1024], P('pipe', 'mp', 'dp')
- grad_gain: float32 [4, 1024], P('pipe', 'mp')
The draws below stay inside these ranges and needn't reach their ends.
All inputs are finite; a program needn't handle non-finite values.
Results may differ from the reference program's by a relative error of at most 0.023.
Values may be sent and summed in bfloat16 or wider, within the bound.
A program may use at most 128 MiB of HBM per device.

```python
import math
import jax
import jax.numpy as jnp
from jax import lax

D = 1024
FF = 32768
MICRO = 4
SEGMENTS = 4
MB_TOK = 128


def shard_levels(rng, shape, split, low, largest):
    def one(dim, shards_of):
        steps = jax.random.uniform(jax.random.fold_in(jax.random.fold_in(rng, 6), dim), (shards_of,), jnp.float32, low / len(split), largest / len(split))
        return jnp.repeat(jnp.exp(steps), shape[dim] // shards_of).reshape((-1,) + (1,) * (len(shape) - dim - 1))

    level = one(*split[0])
    for cut in split[1:]:
        level = level * one(*cut)
    return level


def gaussian(stream_key, extent, scale, most, pieces=(), kind=jnp.bfloat16):
    entries = jax.random.normal(stream_key, extent, jnp.float32) * scale
    if len(pieces) > 0:
        entries = shard_levels(stream_key, extent, pieces, -0.22, 0.18) * entries
    return jnp.clip(entries, min=-most, max=most).astype(kind)


def setup_inputs(seed: int = 0) -> dict:
    streams_of = jax.random.split(jax.random.key(seed), 6)
    inputs = gaussian(streams_of[0], (MICRO, MB_TOK, D), 1.0, 6.0, ((1, 2), (2, 4)))
    cotangent = gaussian(streams_of[1], (MICRO, MB_TOK, D), 1.0, 6.0, ((1, 2), (2, 4)))
    gain = jnp.clip(1.0 + 0.15 * jax.random.normal(streams_of[2], (SEGMENTS, D), jnp.float32), 0.25, 1.75)
    weight_in = gaussian(streams_of[3], (SEGMENTS, D, FF), D ** -0.5, 0.1875, ((0, 4), (2, 4)))
    weight_out = gaussian(streams_of[4], (SEGMENTS, FF, D), FF ** -0.5, 0.03125, ((0, 4), (1, 4)))
    return dict(inputs=inputs, cotangent=cotangent, gain=gain, weight_in=weight_in, weight_out=weight_out)


GELU_COEF = math.sqrt(2.0 / math.pi)
CUBIC_COEF = 0.044715
NORM_EPS = 1e-06

def gelu_parts(values):
    tangent = jnp.tanh(GELU_COEF * (values + CUBIC_COEF * values * values * values))
    output = 0.5 * values * (1.0 + tangent)
    derivative = 0.5 * (1.0 + tangent) + 0.5 * values * (1.0 - tangent * tangent) * GELU_COEF * (1.0 + 3.0 * CUBIC_COEF * values * values)
    return (output, derivative)

def reference(inputs, cotangent, gain, weight_in, weight_out):
    hidden_rows = inputs.reshape(-1, D)
    saved = []
    for segment in range(SEGMENTS):
        values = hidden_rows.astype(jnp.float32)
        inv_rms = lax.rsqrt(lax.optimization_barrier(jnp.mean(values * values, axis=1, keepdims=True)) + NORM_EPS)
        normed = (values * inv_rms * gain[segment]).astype(jnp.bfloat16)
        gate_input = jnp.dot(normed, weight_in[segment], preferred_element_type=jnp.float32)
        activated = gelu_parts(gate_input)[0].astype(jnp.bfloat16)
        branch = jnp.dot(activated, weight_out[segment], preferred_element_type=jnp.float32)
        saved.append((values, inv_rms, normed))
        hidden_rows = (values + branch).astype(jnp.bfloat16)
    grad_rows = cotangent.reshape(-1, D).astype(jnp.float32)
    grads_in = [None] * SEGMENTS
    grads_out = [None] * SEGMENTS
    grads_gain = [None] * SEGMENTS
    for segment in reversed(range(SEGMENTS)):
        values, inv_rms, normed = saved[segment]
        gate_input = jnp.dot(normed, weight_in[segment], preferred_element_type=jnp.float32)
        output_vals, slopes = gelu_parts(gate_input)
        activated = output_vals.astype(jnp.bfloat16)
        out_grad = grad_rows.astype(jnp.bfloat16)
        inner_grad = jnp.dot(out_grad, weight_out[segment].T, preferred_element_type=jnp.float32)
        pre_grad = (inner_grad * slopes).astype(jnp.bfloat16)
        grads_in[segment] = jnp.dot(normed.T, pre_grad, preferred_element_type=jnp.float32).astype(jnp.bfloat16)
        grads_out[segment] = jnp.dot(activated.T, out_grad, preferred_element_type=jnp.float32).astype(jnp.bfloat16)
        norm_grad = jnp.dot(pre_grad, weight_in[segment].T, preferred_element_type=jnp.float32)
        unit_rows = values * inv_rms
        grads_gain[segment] = lax.optimization_barrier(jnp.sum(norm_grad * unit_rows, axis=0))
        scaled = norm_grad * gain[segment]
        row_dot = lax.optimization_barrier(jnp.sum(scaled * unit_rows, axis=1, keepdims=True))
        grad_rows = grad_rows + inv_rms * (scaled - unit_rows * row_dot / D)
    return (jnp.stack(grads_in), jnp.stack(grads_out), jnp.stack(grads_gain))
```

```python
import functools
import math

import jax
import jax.numpy as jnp
from jax import lax
from jax.experimental import pallas as pl
from jax.experimental.pallas import tpu as pltpu
from jax.sharding import PartitionSpec as P

GELU_COEF = math.sqrt(2.0 / math.pi)
CUBIC_COEF = 0.044715
NORM_EPS = 1e-06
CONTRACT_LAST = (((1,), (1,)), ((), ()))
CONTRACT_FIRST = (((0,), (0,)), ((), ()))
MESH = pl.DeviceIdType.MESH


def gelu_parts(values):
    square = values * values
    half = 0.5 + 0.5 * jnp.tanh(values * (GELU_COEF + GELU_COEF * CUBIC_COEF * square))
    bend = values * (half - half * half)
    derivative = half + bend * (2.0 * GELU_COEF + 6.0 * GELU_COEF * CUBIC_COEF * square)
    return (values * half, derivative)


def inverse_rms(values):
    return lax.rsqrt(jnp.mean(values * values, axis=1, keepdims=True) + NORM_EPS)


def relay(
    sizes,
    x_ref,
    cot_ref,
    gain_ref,
    w1_hbm,
    w2_hbm,
    z_out,
    p_out,
    u_out,
    e_out,
    gain_out,
    w1,
    w2,
    z_keep,
    p_keep,
    h_all,
    u_all,
    e_all,
    acc,
    f_send,
    f_recv,
    b_send,
    b_recv,
    h_hop,
    g_hop,
    gain_part,
    gain_recv,
    w1_sem,
    w2_sem,
    z_sem,
    p_sem,
    out_sem,
    x_ssem,
    x_rsem,
    hop_sem,
    ag_ssem,
    ag_rsem,
    dp_ssem,
    dp_rsem,
    rs_ssem,
    rs_rsem,
    gain_ssem,
    gain_rsem,
):
    stages, parts, replicas = sizes
    sec = lax.axis_index("pipe")
    me = lax.axis_index("mp")
    rep = lax.axis_index("dp")
    tiles, full, tile = w1.shape
    rows = h_all.shape[0]
    own = rows // parts
    width = full // parts
    first = sec == 0
    last = sec == stages - 1

    def w_copies(i):
        start = pl.multiple_of(i * tile, tile)
        return (
            pltpu.make_async_copy(w1_hbm.at[:, pl.ds(start, tile)], w1.at[i], w1_sem.at[i]),
            pltpu.make_async_copy(w2_hbm.at[pl.ds(start, tile), :], w2.at[i], w2_sem.at[i]),
        )

    for i in range(tiles):
        for copy in w_copies(i):
            copy.start()

    barrier = pltpu.get_barrier_semaphore()
    peers = []
    for d in range(replicas):
        for j in range(parts):
            if d or j:
                peers.append((d, j, lax.rem(rep + d, replicas), lax.rem(me + j, parts)))
    for _, _, other, part in peers:
        pl.semaphore_signal(
            barrier, inc=1, device_id={"dp": other, "mp": part}, device_id_type=MESH
        )
    for step in (1, stages - 1):
        pl.semaphore_signal(
            barrier,
            inc=1,
            device_id={"pipe": lax.rem(sec + step, stages)},
            device_id_type=MESH,
        )
    pl.semaphore_wait(barrier, len(peers) + 2)

    my_rows = pl.ds(pl.multiple_of(me * own, own), own)
    my_cols = pl.ds(pl.multiple_of(me * width, width), width)

    def remote(src, dst, ssem, rsem, where):
        return pltpu.make_async_remote_copy(
            src_ref=src,
            dst_ref=dst,
            send_sem=ssem,
            recv_sem=rsem,
            device_id=where,
            device_id_type=MESH,
        )

    def others():
        return [(j, lax.rem(me + j, parts)) for j in range(1, parts)]

    def feature_copies(src, dst):
        return [
            remote(src, dst.at[:, my_cols], x_ssem.at[j], x_rsem.at[j], {"mp": part})
            for j, part in others()
        ]

    def row_copies(dst, which):
        return [
            remote(
                dst.at[my_rows, :],
                dst.at[my_rows, :],
                ag_ssem.at[which, j],
                ag_rsem.at[which, j],
                {"mp": part},
            )
            for j, part in others()
        ]

    def sum_copies(src, dst, which):
        return [
            remote(
                src.at[pl.ds(pl.multiple_of(part * own, own), own), :],
                dst.at[j],
                rs_ssem.at[which, j],
                rs_rsem.at[which, j],
                {"mp": part},
            )
            for j, part in others()
        ]

    def replica_copies(ref, which):
        return [
            remote(
                ref.at[0],
                ref.at[d],
                dp_ssem.at[which, d],
                dp_rsem.at[which, d],
                {"dp": lax.rem(rep + d, replicas)},
            )
            for d in range(1, replicas)
        ]

    def start(copies):
        for copy in copies:
            copy.start()

    def finish(copies):
        for copy in copies:
            copy.wait()

    def forward_hop():
        return remote(
            h_hop,
            h_all.at[my_rows, :],
            hop_sem.at[0],
            hop_sem.at[1],
            {"pipe": lax.rem(sec + 1, stages)},
        )

    def backward_hop():
        return remote(
            g_hop,
            e_all.at[0, my_rows, :],
            hop_sem.at[2],
            hop_sem.at[3],
            {"pipe": lax.rem(sec + stages - 1, stages)},
        )

    @pl.when(last)
    def _():
        copies = feature_copies(cot_ref, e_all.at[0])
        start(copies)
        e_all[0, :, my_cols] = cot_ref[...]
        finish(copies)
        start(replica_copies(e_all, 1))

    @pl.when(first)
    def _():
        copies = feature_copies(x_ref, h_all)
        start(copies)
        h_all[:, my_cols] = x_ref[...]
        finish(copies)

    @pl.when(jnp.logical_not(first))
    def _():
        forward_hop().wait_recv()
        copies = row_copies(h_all, 0)
        start(copies)
        finish(copies)

    values = h_all[...].astype(jnp.float32)
    u_all[0] = (values * inverse_rms(values) * gain_ref[...]).astype(jnp.bfloat16)
    start(replica_copies(u_all, 0))
    acc[...] = jnp.zeros_like(acc)

    def z_copy(d, i):
        return pltpu.make_async_copy(
            z_keep.at[d, i],
            z_out.at[pl.ds(d * rows, rows), pl.ds(pl.multiple_of(i * tile, tile), tile)],
            z_sem.at[d, i],
        )

    def p_copy(d, i):
        return pltpu.make_async_copy(
            p_keep.at[d, i],
            p_out.at[pl.ds(d * rows, rows), pl.ds(pl.multiple_of(i * tile, tile), tile)],
            p_sem.at[d, i],
        )

    def activate(d, i):
        gate = jnp.dot(u_all[d], w1[i], preferred_element_type=jnp.float32)
        output, slope = gelu_parts(gate)
        output = output.astype(jnp.bfloat16)
        z_keep[d, i] = output
        p_keep[d, i] = slope.astype(jnp.bfloat16)
        return output

    def pregrad(d, i):
        inner = lax.dot_general(
            e_all[d], w2[i], CONTRACT_LAST, preferred_element_type=jnp.float32
        )
        grad = (inner * p_keep[d, i].astype(jnp.float32)).astype(jnp.bfloat16)
        p_keep[d, i] = grad
        return grad

    @pl.loop(0, tiles)
    def _(i):
        for copy in w_copies(i):
            copy.wait()
        output = activate(0, i)

        @pl.when(jnp.logical_not(last))
        def _():
            acc[...] += jnp.dot(output, w2[i], preferred_element_type=jnp.float32)

    @pl.when(jnp.logical_not(last))
    def _():
        f_send[...] = acc[...].astype(jnp.bfloat16)
        copies = sum_copies(f_send, f_recv, 0)
        start(copies)
        total = h_all[my_rows, :].astype(jnp.float32) + acc[my_rows, :]
        for j, copy in enumerate(copies):
            copy.wait()
            total += f_recv[j + 1].astype(jnp.float32)
        h_hop[...] = total.astype(jnp.bfloat16)
        forward_hop().start()

    @pl.loop(0, tiles)
    def _(i):
        z_copy(0, i).start()

    def replica_forward():
        finish(replica_copies(u_all, 0))
        for d in range(1, replicas):

            @pl.loop(0, tiles)
            def _(i):
                activate(d, i)
                z_copy(d, i).start()

    @pl.when(jnp.logical_not(last))
    def _():
        replica_forward()
        forward_hop().wait_send()
        backward_hop().wait_recv()
        copies = row_copies(e_all.at[0], 1)
        start(copies)
        finish(copies)
        start(replica_copies(e_all, 1))

    acc[...] = jnp.zeros_like(acc)

    @pl.loop(0, tiles)
    def _(i):
        grad = pregrad(0, i)
        acc[...] += lax.dot_general(
            grad, w1[i], CONTRACT_LAST, preferred_element_type=jnp.float32
        )
        p_copy(0, i).start()

    @pl.when(jnp.logical_not(first))
    def _():
        b_send[...] = acc[...].astype(jnp.bfloat16)
        copies = sum_copies(b_send, b_recv, 1)
        start(copies)
        mine = h_all[my_rows, :].astype(jnp.float32)
        scale = inverse_rms(mine)
        unit = mine * scale
        total = acc[my_rows, :]
        for j, copy in enumerate(copies):
            copy.wait()
            total += b_recv[j + 1].astype(jnp.float32)
        scaled = total * gain_ref[...]
        row_dot = jnp.sum(scaled * unit, axis=1, keepdims=True)
        previous = e_all[0, my_rows, :].astype(jnp.float32) + scale * (
            scaled - unit * (row_dot / full)
        )
        g_hop[...] = previous.astype(jnp.bfloat16)
        backward_hop().start()

    values = h_all[...].astype(jnp.float32)
    terms = acc[...] * (values * inverse_rms(values))
    gain_part[...] = jnp.sum(terms.reshape(rows // 8, 8, full), axis=0)
    gain_copies = [
        remote(
            gain_part.at[:, pl.ds(pl.multiple_of(part * width, width), width)],
            gain_recv.at[d * parts + j],
            gain_ssem.at[d * parts + j],
            gain_rsem.at[d * parts + j],
            {"dp": other, "mp": part},
        )
        for d, j, other, part in peers
    ]
    start(gain_copies)

    @pl.when(last)
    def _():
        replica_forward()

    finish(replica_copies(e_all, 1))
    for d in range(1, replicas):

        @pl.loop(0, tiles)
        def _(i):
            pregrad(d, i)
            p_copy(d, i).start()

    outs = []
    for d in range(replicas):
        place = pl.ds(d * rows, rows)
        outs.append(pltpu.make_async_copy(u_all.at[d], u_out.at[place, :], out_sem.at[0, d]))
        outs.append(pltpu.make_async_copy(e_all.at[d], e_out.at[place, :], out_sem.at[1, d]))
    start(outs)
    total = gain_part[:, my_cols]
    for (d, j, _, _), copy in zip(peers, gain_copies):
        copy.wait()
        total += gain_recv[d * parts + j]
    gain_out[...] = jnp.sum(total, axis=0, keepdims=True)

    for d in range(replicas):

        @pl.loop(0, tiles)
        def _(i):
            z_copy(d, i).wait()
            p_copy(d, i).wait()

    finish(outs)

    @pl.when(jnp.logical_not(first))
    def _():
        backward_hop().wait_send()


def shards(inputs, cotangent, gain, weight_in, weight_out):
    stages = lax.axis_size("pipe")
    parts = lax.axis_size("mp")
    replicas = lax.axis_size("dp")
    micro, row_count, width = inputs.shape
    rows = micro * row_count
    full = gain.shape[1]
    hidden = weight_in.shape[2]
    tile = math.gcd(hidden, 1024)
    tiles = hidden // tile
    own = rows // parts
    half = full // replicas
    bf16, f32 = jnp.bfloat16, jnp.float32
    vmem = pl.BlockSpec(memory_space=pltpu.VMEM)
    anywhere = pl.BlockSpec(memory_space=pl.ANY)
    dma = pltpu.SemaphoreType.DMA
    z_all, p_all, u_all, e_all, gain_total = pl.pallas_call(
        functools.partial(relay, (stages, parts, replicas)),
        name="relay",
        out_shape=(
            jax.ShapeDtypeStruct((replicas * rows, hidden), bf16),
            jax.ShapeDtypeStruct((replicas * rows, hidden), bf16),
            jax.ShapeDtypeStruct((replicas * rows, full), bf16),
            jax.ShapeDtypeStruct((replicas * rows, full), bf16),
            jax.ShapeDtypeStruct((1, width), f32),
        ),
        in_specs=[vmem, vmem, vmem, anywhere, anywhere],
        out_specs=(anywhere, anywhere, anywhere, anywhere, vmem),
        scratch_shapes=[
            pltpu.VMEM((tiles, full, tile), bf16),
            pltpu.VMEM((tiles, tile, full), bf16),
            pltpu.VMEM((replicas, tiles, rows, tile), bf16),
            pltpu.VMEM((replicas, tiles, rows, tile), bf16),
            pltpu.VMEM((rows, full), bf16),
            pltpu.VMEM((replicas, rows, full), bf16),
            pltpu.VMEM((replicas, rows, full), bf16),
            pltpu.VMEM((rows, full), f32),
            pltpu.VMEM((rows, full), bf16),
            pltpu.VMEM((parts, own, full), bf16),
            pltpu.VMEM((rows, full), bf16),
            pltpu.VMEM((parts, own, full), bf16),
            pltpu.VMEM((own, full), bf16),
            pltpu.VMEM((own, full), bf16),
            pltpu.VMEM((8, full), f32),
            pltpu.VMEM((replicas * parts, 8, width), f32),
            dma((tiles,)),
            dma((tiles,)),
            dma((replicas, tiles)),
            dma((replicas, tiles)),
            dma((2, replicas)),
            dma((parts,)),
            dma((parts,)),
            dma((4,)),
            dma((2, parts)),
            dma((2, parts)),
            dma((2, replicas)),
            dma((2, replicas)),
            dma((2, parts)),
            dma((2, parts)),
            dma((replicas * parts,)),
            dma((replicas * parts,)),
        ],
        compiler_params=pltpu.CompilerParams(
            collective_id=0, has_side_effects=True, vmem_limit_bytes=67043328
        ),
    )(
        inputs.reshape(rows, width),
        cotangent.reshape(rows, width),
        gain,
        weight_in[0],
        weight_out[0],
    )
    begin = lax.axis_index("dp") * half
    u_cols = lax.dynamic_slice_in_dim(u_all, begin, half, 1)
    e_cols = lax.dynamic_slice_in_dim(e_all, begin, half, 1)
    grad_first = lax.dot_general(u_cols, p_all, CONTRACT_FIRST, preferred_element_type=f32)
    grad_second = lax.dot_general(z_all, e_cols, CONTRACT_FIRST, preferred_element_type=f32)
    return (grad_first.astype(bf16)[None], grad_second.astype(bf16)[None], gain_total)


def solution(mesh):
    in_specs = (
        P(None, "dp", "mp"),
        P(None, "dp", "mp"),
        P("pipe", None),
        P("pipe", None, "mp"),
        P("pipe", "mp", None),
    )
    out_specs = (P("pipe", "dp", "mp"), P("pipe", "mp", "dp"), P("pipe", "mp"))
    return jax.shard_map(shards, mesh=mesh, in_specs=in_specs, out_specs=out_specs, check_vma=False)
```

```python
import functools
import math

import jax
import jax.numpy as jnp
from jax import lax
from jax.experimental import pallas as pl
from jax.experimental.pallas import tpu as pltpu
from jax.sharding import PartitionSpec as P

GELU_COEF = math.sqrt(2.0 / math.pi)
CUBIC_COEF = 0.044715
NORM_EPS = 1e-06
CONTRACT_LAST = (((1,), (1,)), ((), ()))
CONTRACT_FIRST = (((0,), (0,)), ((), ()))
MESH = pl.DeviceIdType.MESH


def gelu_parts(values):
    square = values * values
    half = 0.5 + 0.5 * jnp.tanh(values * (GELU_COEF + GELU_COEF * CUBIC_COEF * square))
    bend = values * (half - half * half)
    derivative = half + bend * (2.0 * GELU_COEF + 6.0 * GELU_COEF * CUBIC_COEF * square)
    return (values * half, derivative)


def inverse_rms(values):
    return lax.rsqrt(jnp.mean(values * values, axis=1, keepdims=True) + NORM_EPS)


def relay(
    sizes,
    x_ref,
    cot_ref,
    gain_ref,
    w1_hbm,
    w2_hbm,
    z_out,
    p_out,
    ut_out,
    e_out,
    gain_out,
    w1,
    w2,
    z_keep,
    p_keep,
    h_all,
    u_all,
    ut,
    e_all,
    acc,
    f_send,
    f_recv,
    b_send,
    b_recv,
    h_hop,
    g_hop,
    gain_part,
    gain_recv,
    w1_sem,
    w2_sem,
    z_sem,
    p_sem,
    out_sem,
    x_ssem,
    x_rsem,
    hop_sem,
    ag_ssem,
    ag_rsem,
    dp_ssem,
    dp_rsem,
    rs_ssem,
    rs_rsem,
    gain_ssem,
    gain_rsem,
):
    stages, parts, replicas, hop_width = sizes
    sec = lax.axis_index("pipe")
    me = lax.axis_index("mp")
    rep = lax.axis_index("dp")
    tiles, full, tile = w1.shape
    rows = h_all.shape[0]
    own = rows // parts
    width = full // parts
    chunks = f_send.shape[1] // hop_width
    first = sec == 0
    last = sec == stages - 1

    def w_copies(i):
        start = pl.multiple_of(i * tile, tile)
        return (
            pltpu.make_async_copy(w1_hbm.at[:, pl.ds(start, tile)], w1.at[i], w1_sem.at[i]),
            pltpu.make_async_copy(w2_hbm.at[pl.ds(start, tile), :], w2.at[i], w2_sem.at[i]),
        )

    for which in range(2):
        for i in range(tiles):
            w_copies(i)[which].start()

    barrier = pltpu.get_barrier_semaphore()
    peers = []
    for d in range(replicas):
        for j in range(parts):
            if d or j:
                peers.append((d, j, lax.rem(rep + d, replicas), lax.rem(me + j, parts)))
    for _, _, other, part in peers:
        pl.semaphore_signal(
            barrier, inc=1, device_id={"dp": other, "mp": part}, device_id_type=MESH
        )
    for step in (1, stages - 1):
        pl.semaphore_signal(
            barrier,
            inc=1,
            device_id={"pipe": lax.rem(sec + step, stages)},
            device_id_type=MESH,
        )
    pl.semaphore_wait(barrier, len(peers) + 2)

    my_rows = pl.ds(pl.multiple_of(me * own, own), own)
    my_cols = pl.ds(pl.multiple_of(me * width, width), width)

    def remote(src, dst, ssem, rsem, where):
        return pltpu.make_async_remote_copy(
            src_ref=src,
            dst_ref=dst,
            send_sem=ssem,
            recv_sem=rsem,
            device_id=where,
            device_id_type=MESH,
        )

    def others():
        return [(j, lax.rem(me + j, parts)) for j in range(1, parts)]

    def feature_copies(src, dst):
        return [
            remote(src, dst.at[:, my_cols], x_ssem.at[j], x_rsem.at[j], {"mp": part})
            for j, part in others()
        ]

    chips = parts // 2
    chip, core = me // 2, lax.rem(me, 2)
    mate = chip * 2 + 1 - core

    def columns(q):
        return pl.ds(pl.multiple_of(q * hop_width, hop_width), hop_width)

    def block_rows(k):
        block = lax.rem(chip + chips - k, chips) * 2 + core
        return pl.ds(pl.multiple_of(block * own, own), own)

    def chip_copy(ref, which, q, k):
        part = ref.at[my_rows, columns(q)]
        target = lax.rem(chip + k, chips) * 2 + core
        return remote(
            part, part, ag_ssem.at[which, q, k], ag_rsem.at[which, q, k], {"mp": target}
        )

    def mate_copy(ref, which, q, k):
        part = ref.at[block_rows(k), columns(q)]
        slot = chips + k
        return remote(
            part, part, ag_ssem.at[which, q, slot], ag_rsem.at[which, q, slot], {"mp": mate}
        )

    def gather(ref, which, hop):
        for q in range(chunks):
            hop(q).wait_recv()
            for k in range(1, chips):
                chip_copy(ref, which, q, k).start()
            mate_copy(ref, which, q, 0).start()
        for q in range(chunks):
            for k in range(1, chips):
                chip_copy(ref, which, q, k).wait_recv()
                mate_copy(ref, which, q, k).start()
        for q in range(chunks):
            for k in range(1, chips):
                chip_copy(ref, which, q, k).wait_send()
            for k in range(chips):
                mate_copy(ref, which, q, k).wait()

    def sum_copies(src, dst, which, q):
        return [
            remote(
                src.at[pl.ds(pl.multiple_of(part * own, own), own), columns(q)],
                dst.at[j, :, columns(q)],
                rs_ssem.at[which, q, j],
                rs_rsem.at[which, q, j],
                {"mp": part},
            )
            for j, part in others()
        ]

    def replica_copies(ref, which):
        return [
            remote(
                ref.at[0],
                ref.at[d],
                dp_ssem.at[which, d],
                dp_rsem.at[which, d],
                {"dp": lax.rem(rep + d, replicas)},
            )
            for d in range(1, replicas)
        ]

    def start(copies):
        for copy in copies:
            copy.start()

    def finish(copies):
        for copy in copies:
            copy.wait()

    def forward_hop(q):
        return remote(
            h_hop.at[:, columns(q)],
            h_all.at[my_rows, columns(q)],
            hop_sem.at[0, q],
            hop_sem.at[1, q],
            {"pipe": lax.rem(sec + 1, stages)},
        )

    def backward_hop(q):
        return remote(
            g_hop.at[:, columns(q)],
            e_all.at[0, my_rows, columns(q)],
            hop_sem.at[2, q],
            hop_sem.at[3, q],
            {"pipe": lax.rem(sec + stages - 1, stages)},
        )

    step_width = math.gcd(tile, 256)
    steps = tile // step_width

    def staged(product, use):
        held = product(0)
        for s in range(1, steps):
            ahead = product(s)
            use(s - 1, held)
            held = ahead
        use(steps - 1, held)

    def activate(d, i, scaled=False):
        def product(s):
            piece = w1[i, :, s * step_width : (s + 1) * step_width]
            return jnp.dot(u_all[d], piece, preferred_element_type=jnp.float32)

        def use(s, gate):
            place = slice(s * step_width, (s + 1) * step_width)
            output, slope = gelu_parts(gate)
            z_keep[d, i, :, place] = output.astype(jnp.bfloat16)
            if scaled:
                slope = slope * p_keep[d, i, :, place].astype(jnp.float32)
            p_keep[d, i, :, place] = slope.astype(jnp.bfloat16)

        staged(product, use)

    def pregrad(d, i, scaled=True):
        def product(s):
            piece = w2[i, s * step_width : (s + 1) * step_width, :]
            return lax.dot_general(
                e_all[d], piece, CONTRACT_LAST, preferred_element_type=jnp.float32
            )

        def use(s, inner):
            place = slice(s * step_width, (s + 1) * step_width)
            if scaled:
                inner = inner * p_keep[d, i, :, place].astype(jnp.float32)
            p_keep[d, i, :, place] = inner.astype(jnp.bfloat16)

        staged(product, use)

    @pl.when(last)
    def _():
        copies = feature_copies(cot_ref, e_all.at[0])
        start(copies)
        e_all[0, :, my_cols] = cot_ref[...]
        finish(copies)
        start(replica_copies(e_all, 1))

        @pl.loop(0, tiles)
        def _(i):
            w_copies(i)[1].wait()
            pregrad(0, i, scaled=False)

    @pl.when(first)
    def _():
        copies = feature_copies(x_ref, h_all)
        start(copies)
        h_all[:, my_cols] = x_ref[...]
        finish(copies)

    @pl.when(jnp.logical_not(first))
    def _():
        gather(h_all, 0, forward_hop)

    values = h_all[...].astype(jnp.float32)
    u_all[0] = (values * inverse_rms(values) * gain_ref[...]).astype(jnp.bfloat16)
    start(replica_copies(u_all, 0))

    def z_copy(d, i):
        return pltpu.make_async_copy(
            z_keep.at[d, i],
            z_out.at[pl.ds(d * rows, rows), pl.ds(pl.multiple_of(i * tile, tile), tile)],
            z_sem.at[d, i],
        )

    def p_copy(d, i):
        return pltpu.make_async_copy(
            p_keep.at[d, i],
            p_out.at[pl.ds(d * rows, rows), pl.ds(pl.multiple_of(i * tile, tile), tile)],
            p_sem.at[d, i],
        )

    @pl.when(last)
    def _():
        @pl.loop(0, tiles)
        def _(i):
            w_copies(i)[0].wait()
            activate(0, i, scaled=True)
            p_copy(0, i).start()

    def pass_on(q):
        total = h_all[my_rows, columns(q)].astype(jnp.float32) + acc[my_rows, columns(q)]
        for j, copy in enumerate(sum_copies(f_send, f_recv, 0, q)):
            copy.wait()
            total += f_recv[j + 1, :, columns(q)].astype(jnp.float32)
        h_hop[:, columns(q)] = total.astype(jnp.bfloat16)
        forward_hop(q).start()

    @pl.when(jnp.logical_not(last))
    def _():
        @pl.loop(0, tiles)
        def _(i):
            w_copies(i)[0].wait()
            activate(0, i)

        @pl.loop(0, tiles)
        def _(i):
            w_copies(i)[1].wait()

        @pl.loop(0, chunks)
        def _(q):
            total = jnp.zeros((rows, hop_width), jnp.float32)
            for i in range(tiles):
                total += jnp.dot(
                    z_keep[0, i], w2[i, :, columns(q)], preferred_element_type=jnp.float32
                )
            acc[:, columns(q)] = total
            f_send[:, columns(q)] = total.astype(jnp.bfloat16)
            start(sum_copies(f_send, f_recv, 0, q))

            @pl.when(q > 0)
            def _():
                pass_on(q - 1)

        pass_on(chunks - 1)

    @pl.loop(0, tiles)
    def _(i):
        z_copy(0, i).start()

    def replica_forward():
        finish(replica_copies(u_all, 0))
        for d in range(1, replicas):

            @pl.loop(0, tiles)
            def _(i):
                activate(d, i)
                z_copy(d, i).start()

        half = full // replicas
        kept = pl.ds(pl.multiple_of(rep * half, half), half)
        for d in range(replicas):
            flipped = u_all[d, :, kept].astype(jnp.float32).T
            ut[:, d * rows : (d + 1) * rows] = flipped.astype(jnp.bfloat16)
        pltpu.make_async_copy(ut, ut_out, out_sem.at[0, 0]).start()

    @pl.when(jnp.logical_not(last))
    def _():
        replica_forward()
        for q in range(chunks):
            forward_hop(q).wait_send()
        gather(e_all.at[0], 1, backward_hop)
        start(replica_copies(e_all, 1))

        @pl.loop(0, tiles)
        def _(i):
            pregrad(0, i)
            p_copy(0, i).start()

    @pl.loop(0, chunks)
    def _(q):
        total = jnp.zeros((rows, hop_width), jnp.float32)
        for i in range(tiles):
            total += lax.dot_general(
                p_keep[0, i], w1[i, columns(q), :], CONTRACT_LAST, preferred_element_type=jnp.float32
            )
        acc[:, columns(q)] = total

        @pl.when(jnp.logical_not(first))
        def _():
            b_send[:, columns(q)] = total.astype(jnp.bfloat16)
            start(sum_copies(b_send, b_recv, 1, q))

    @pl.when(jnp.logical_not(first))
    def _():
        mine = h_all[my_rows, :].astype(jnp.float32)
        scale = inverse_rms(mine)
        unit = mine * scale
        total = acc[my_rows, :]
        for q in range(chunks):
            finish(sum_copies(b_send, b_recv, 1, q))
        for j in range(1, parts):
            total += b_recv[j].astype(jnp.float32)
        scaled = total * gain_ref[...]
        row_dot = jnp.sum(scaled * unit, axis=1, keepdims=True)
        previous = e_all[0, my_rows, :].astype(jnp.float32) + scale * (
            scaled - unit * (row_dot / full)
        )
        g_hop[...] = previous.astype(jnp.bfloat16)
        for q in range(chunks):
            backward_hop(q).start()

    values = h_all[...].astype(jnp.float32)
    terms = acc[...] * (values * inverse_rms(values))
    gain_part[...] = jnp.sum(terms.reshape(rows // 8, 8, full), axis=0)
    gain_copies = [
        remote(
            gain_part.at[:, pl.ds(pl.multiple_of(part * width, width), width)],
            gain_recv.at[d * parts + j],
            gain_ssem.at[d * parts + j],
            gain_rsem.at[d * parts + j],
            {"dp": other, "mp": part},
        )
        for d, j, other, part in peers
    ]
    start(gain_copies)

    @pl.when(last)
    def _():
        replica_forward()

    finish(replica_copies(e_all, 1))
    for d in range(1, replicas):

        @pl.loop(0, tiles)
        def _(i):
            pregrad(d, i)
            p_copy(d, i).start()

    outs = []
    for d in range(replicas):
        place = pl.ds(d * rows, rows)
        outs.append(pltpu.make_async_copy(e_all.at[d], e_out.at[place, :], out_sem.at[1, d]))
    start(outs)
    outs.append(pltpu.make_async_copy(ut, ut_out, out_sem.at[0, 0]))
    total = gain_part[:, my_cols]
    for (d, j, _, _), copy in zip(peers, gain_copies):
        copy.wait()
        total += gain_recv[d * parts + j]
    gain_out[...] = jnp.sum(total, axis=0, keepdims=True)

    for d in range(replicas):

        @pl.loop(0, tiles)
        def _(i):
            z_copy(d, i).wait()
            p_copy(d, i).wait()

    finish(outs)

    @pl.when(jnp.logical_not(first))
    def _():
        for q in range(chunks):
            backward_hop(q).wait_send()


def shards(inputs, cotangent, gain, weight_in, weight_out):
    stages = lax.axis_size("pipe")
    parts = lax.axis_size("mp")
    replicas = lax.axis_size("dp")
    micro, row_count, width = inputs.shape
    rows = micro * row_count
    full = gain.shape[1]
    hidden = weight_in.shape[2]
    tile = math.gcd(hidden, 1024)
    tiles = hidden // tile
    own = rows // parts
    half = full // replicas
    hop_width = math.gcd(full, 256)
    chunks = full // hop_width
    bf16, f32 = jnp.bfloat16, jnp.float32
    vmem = pl.BlockSpec(memory_space=pltpu.VMEM)
    anywhere = pl.BlockSpec(memory_space=pl.ANY)
    dma = pltpu.SemaphoreType.DMA
    z_all, p_all, u_flip, e_all, gain_total = pl.pallas_call(
        functools.partial(relay, (stages, parts, replicas, hop_width)),
        name="relay",
        out_shape=(
            jax.ShapeDtypeStruct((replicas * rows, hidden), bf16),
            jax.ShapeDtypeStruct((replicas * rows, hidden), bf16),
            jax.ShapeDtypeStruct((half, replicas * rows), bf16),
            jax.ShapeDtypeStruct((replicas * rows, full), bf16),
            jax.ShapeDtypeStruct((1, width), f32),
        ),
        in_specs=[vmem, vmem, vmem, anywhere, anywhere],
        out_specs=(anywhere, anywhere, anywhere, anywhere, vmem),
        scratch_shapes=[
            pltpu.VMEM((tiles, full, tile), bf16),
            pltpu.VMEM((tiles, tile, full), bf16),
            pltpu.VMEM((replicas, tiles, rows, tile), bf16),
            pltpu.VMEM((replicas, tiles, rows, tile), bf16),
            pltpu.VMEM((rows, full), bf16),
            pltpu.VMEM((replicas, rows, full), bf16),
            pltpu.VMEM((half, replicas * rows), bf16),
            pltpu.VMEM((replicas, rows, full), bf16),
            pltpu.VMEM((rows, full), f32),
            pltpu.VMEM((rows, full), bf16),
            pltpu.VMEM((parts, own, full), bf16),
            pltpu.VMEM((rows, full), bf16),
            pltpu.VMEM((parts, own, full), bf16),
            pltpu.VMEM((own, full), bf16),
            pltpu.VMEM((own, full), bf16),
            pltpu.VMEM((8, full), f32),
            pltpu.VMEM((replicas * parts, 8, width), f32),
            dma((tiles,)),
            dma((tiles,)),
            dma((replicas, tiles)),
            dma((replicas, tiles)),
            dma((2, replicas)),
            dma((parts,)),
            dma((parts,)),
            dma((4, chunks)),
            dma((2, chunks, parts)),
            dma((2, chunks, parts)),
            dma((2, replicas)),
            dma((2, replicas)),
            dma((2, chunks, parts)),
            dma((2, chunks, parts)),
            dma((replicas * parts,)),
            dma((replicas * parts,)),
        ],
        compiler_params=pltpu.CompilerParams(
            collective_id=0, has_side_effects=True, vmem_limit_bytes=67043328
        ),
    )(
        inputs.reshape(rows, width),
        cotangent.reshape(rows, width),
        gain,
        weight_in[0],
        weight_out[0],
    )
    begin = lax.axis_index("dp") * half
    e_cols = lax.dynamic_slice_in_dim(e_all, begin, half, 1)
    grad_first = jnp.dot(u_flip, p_all, preferred_element_type=f32)
    grad_second = lax.dot_general(z_all, e_cols, CONTRACT_FIRST, preferred_element_type=f32)
    return (grad_first.astype(bf16)[None], grad_second.astype(bf16)[None], gain_total)


def solution(mesh):
    in_specs = (
        P(None, "dp", "mp"),
        P(None, "dp", "mp"),
        P("pipe", None),
        P("pipe", None, "mp"),
        P("pipe", "mp", None),
    )
    out_specs = (P("pipe", "dp", "mp"), P("pipe", "mp", "dp"), P("pipe", "mp"))
    return jax.shard_map(shards, mesh=mesh, in_specs=in_specs, out_specs=out_specs, check_vma=False)
```

```python
import functools
import math

import jax
import jax.numpy as jnp
from jax import lax
from jax.experimental import pallas as pl
from jax.experimental.pallas import tpu as pltpu
from jax.sharding import PartitionSpec as P

GELU_COEF = math.sqrt(2.0 / math.pi)
CUBIC_COEF = 0.044715
NORM_EPS = 1e-06
CONTRACT_LAST = (((1,), (1,)), ((), ()))
CONTRACT_FIRST = (((0,), (0,)), ((), ()))
MESH = pl.DeviceIdType.MESH


def gelu_parts(values):
    square = values * values
    half = 0.5 + 0.5 * jnp.tanh(values * (GELU_COEF + GELU_COEF * CUBIC_COEF * square))
    bend = values * (half - half * half)
    derivative = half + bend * (2.0 * GELU_COEF + 6.0 * GELU_COEF * CUBIC_COEF * square)
    return (values * half, derivative)


def inverse_rms(values):
    return lax.rsqrt(jnp.mean(values * values, axis=1, keepdims=True) + NORM_EPS)


def relay(
    sizes,
    x_ref,
    cot_ref,
    gain_ref,
    w1_hbm,
    w2_hbm,
    z_out,
    p_out,
    ut_out,
    e_out,
    gain_out,
    w1,
    w2,
    z_keep,
    p_keep,
    h_all,
    u_all,
    ut,
    e_all,
    acc,
    f_send,
    f_recv,
    b_send,
    b_recv,
    h_hop,
    g_hop,
    gain_part,
    gain_recv,
    w1_sem,
    w2_sem,
    z_sem,
    p_sem,
    out_sem,
    x_ssem,
    x_rsem,
    hop_sem,
    ag_ssem,
    ag_rsem,
    dp_ssem,
    dp_rsem,
    rs_ssem,
    rs_rsem,
    gain_ssem,
    gain_rsem,
):
    stages, parts, replicas, hop_width = sizes
    sec = lax.axis_index("pipe")
    me = lax.axis_index("mp")
    rep = lax.axis_index("dp")
    tiles, full, tile = w1.shape
    rows = h_all.shape[0]
    own = rows // parts
    width = full // parts
    chunks = f_send.shape[1] // hop_width
    first = sec == 0
    last = sec == stages - 1

    def w_copies(i):
        start = pl.multiple_of(i * tile, tile)
        return (
            pltpu.make_async_copy(w1_hbm.at[:, pl.ds(start, tile)], w1.at[i], w1_sem.at[i]),
            pltpu.make_async_copy(w2_hbm.at[pl.ds(start, tile), :], w2.at[i], w2_sem.at[i]),
        )

    for which in range(2):
        for i in range(tiles):
            w_copies(i)[which].start()

    barrier = pltpu.get_barrier_semaphore()
    peers = []
    for d in range(replicas):
        for j in range(parts):
            if d or j:
                peers.append((d, j, lax.rem(rep + d, replicas), lax.rem(me + j, parts)))
    for _, _, other, part in peers:
        pl.semaphore_signal(
            barrier, inc=1, device_id={"dp": other, "mp": part}, device_id_type=MESH
        )
    for step in (1, stages - 1):
        pl.semaphore_signal(
            barrier,
            inc=1,
            device_id={"pipe": lax.rem(sec + step, stages)},
            device_id_type=MESH,
        )
    pl.semaphore_wait(barrier, len(peers) + 2)

    my_rows = pl.ds(pl.multiple_of(me * own, own), own)
    my_cols = pl.ds(pl.multiple_of(me * width, width), width)

    half = full // replicas
    kept = pl.ds(pl.multiple_of(rep * half, half), half)

    def remote(src, dst, ssem, rsem, where):
        return pltpu.make_async_remote_copy(
            src_ref=src,
            dst_ref=dst,
            send_sem=ssem,
            recv_sem=rsem,
            device_id=where,
            device_id_type=MESH,
        )

    def others():
        return [(j, lax.rem(me + j, parts)) for j in range(1, parts)]

    chips = parts // 2
    chip, core = me // 2, lax.rem(me, 2)
    mate = chip * 2 + 1 - core

    def columns(q):
        return pl.ds(pl.multiple_of(q * hop_width, hop_width), hop_width)

    def block_rows(k):
        block = lax.rem(chip + chips - k, chips) * 2 + core
        return pl.ds(pl.multiple_of(block * own, own), own)

    def chip_copy(ref, which, q, k):
        part = ref.at[my_rows, columns(q)]
        target = lax.rem(chip + k, chips) * 2 + core
        return remote(
            part, part, ag_ssem.at[which, q, k], ag_rsem.at[which, q, k], {"mp": target}
        )

    def mate_copy(ref, which, q, k):
        part = ref.at[block_rows(k), columns(q)]
        slot = chips + k
        return remote(
            part, part, ag_ssem.at[which, q, slot], ag_rsem.at[which, q, slot], {"mp": mate}
        )

    def gather_features(src, dst):
        def cols(k):
            block = lax.rem(chip + chips - k, chips) * 2 + core
            return pl.ds(pl.multiple_of(block * width, width), width)

        def across(k):
            target = lax.rem(chip + k, chips) * 2 + core
            return remote(src, dst.at[:, my_cols], x_ssem.at[k], x_rsem.at[k], {"mp": target})

        def beside(k):
            part = dst.at[:, cols(k)]
            slot = chips + k
            return remote(
                src if k == 0 else part, part, x_ssem.at[slot], x_rsem.at[slot], {"mp": mate}
            )

        for k in range(1, chips):
            across(k).start()
        beside(0).start()
        dst[:, my_cols] = src[...]
        for k in range(1, chips):
            across(k).wait_recv()
            beside(k).start()
        for k in range(1, chips):
            across(k).wait_send()
        for k in range(chips):
            beside(k).wait()

    def gather(ref, which, hop):
        for q in range(chunks):
            hop(q).wait_recv()
            for k in range(1, chips):
                chip_copy(ref, which, q, k).start()
            mate_copy(ref, which, q, 0).start()
        for q in range(chunks):
            for k in range(1, chips):
                chip_copy(ref, which, q, k).wait_recv()
                mate_copy(ref, which, q, k).start()
        for q in range(chunks):
            for k in range(1, chips):
                chip_copy(ref, which, q, k).wait_send()
            for k in range(chips):
                mate_copy(ref, which, q, k).wait()

    def sum_copies(src, dst, which, q):
        return [
            remote(
                src.at[pl.ds(pl.multiple_of(part * own, own), own), columns(q)],
                dst.at[j, :, columns(q)],
                rs_ssem.at[which, q, j],
                rs_rsem.at[which, q, j],
                {"mp": part},
            )
            for j, part in others()
        ]

    def replica_copies(ref, which):
        return [
            remote(
                ref.at[0],
                ref.at[d],
                dp_ssem.at[which, d],
                dp_rsem.at[which, d],
                {"dp": lax.rem(rep + d, replicas)},
            )
            for d in range(1, replicas)
        ]

    def start(copies):
        for copy in copies:
            copy.start()

    def finish(copies):
        for copy in copies:
            copy.wait()

    def forward_hop(q):
        return remote(
            h_hop.at[:, columns(q)],
            h_all.at[my_rows, columns(q)],
            hop_sem.at[0, q],
            hop_sem.at[1, q],
            {"pipe": lax.rem(sec + 1, stages)},
        )

    def backward_hop(q):
        return remote(
            g_hop.at[:, columns(q)],
            e_all.at[0, my_rows, columns(q)],
            hop_sem.at[2, q],
            hop_sem.at[3, q],
            {"pipe": lax.rem(sec + stages - 1, stages)},
        )

    step_width = math.gcd(tile, 256)
    steps = tile // step_width

    def staged(product, use):
        held = product(0)
        for s in range(1, steps):
            ahead = product(s)
            use(s - 1, held)
            held = ahead
        use(steps - 1, held)

    def activate(d, i, scaled=False):
        def product(s):
            piece = w1[i, :, s * step_width : (s + 1) * step_width]
            return jnp.dot(u_all[d], piece, preferred_element_type=jnp.float32)

        def use(s, gate):
            place = slice(s * step_width, (s + 1) * step_width)
            output, slope = gelu_parts(gate)
            z_keep[d, i, :, place] = output.astype(jnp.bfloat16)
            if scaled:
                slope = slope * p_keep[d, i, :, place].astype(jnp.float32)
            p_keep[d, i, :, place] = slope.astype(jnp.bfloat16)

        staged(product, use)

    def pregrad(d, i, scaled=True):
        def product(s):
            piece = w2[i, s * step_width : (s + 1) * step_width, :]
            return lax.dot_general(
                e_all[d], piece, CONTRACT_LAST, preferred_element_type=jnp.float32
            )

        def use(s, inner):
            place = slice(s * step_width, (s + 1) * step_width)
            if scaled:
                inner = inner * p_keep[d, i, :, place].astype(jnp.float32)
            p_keep[d, i, :, place] = inner.astype(jnp.bfloat16)

        staged(product, use)

    @pl.when(last)
    def _():
        gather_features(cot_ref, e_all.at[0])
        start(replica_copies(e_all, 1))

        @pl.loop(0, tiles)
        def _(i):
            w_copies(i)[1].wait()
            pregrad(0, i, scaled=False)

    @pl.when(first)
    def _():
        gather_features(x_ref, h_all)

    @pl.when(jnp.logical_not(first))
    def _():
        gather(h_all, 0, forward_hop)

    values = h_all[...].astype(jnp.float32)
    u_all[0] = (values * inverse_rms(values) * gain_ref[...]).astype(jnp.bfloat16)
    start(replica_copies(u_all, 0))

    def z_copy(d, i):
        return pltpu.make_async_copy(
            z_keep.at[d, i],
            z_out.at[pl.ds(d * rows, rows), pl.ds(pl.multiple_of(i * tile, tile), tile)],
            z_sem.at[d, i],
        )

    def p_copy(d, i):
        return pltpu.make_async_copy(
            p_keep.at[d, i],
            p_out.at[pl.ds(d * rows, rows), pl.ds(pl.multiple_of(i * tile, tile), tile)],
            p_sem.at[d, i],
        )

    @pl.when(last)
    def _():
        @pl.loop(0, tiles)
        def _(i):
            w_copies(i)[0].wait()
            activate(0, i, scaled=True)
            p_copy(0, i).start()

    def pass_on(q):
        total = h_all[my_rows, columns(q)].astype(jnp.float32) + acc[my_rows, columns(q)]
        for j, copy in enumerate(sum_copies(f_send, f_recv, 0, q)):
            copy.wait()
            total += f_recv[j + 1, :, columns(q)].astype(jnp.float32)
        h_hop[:, columns(q)] = total.astype(jnp.bfloat16)
        forward_hop(q).start()

    @pl.when(jnp.logical_not(last))
    def _():
        @pl.loop(0, tiles)
        def _(i):
            w_copies(i)[0].wait()
            activate(0, i)

        @pl.loop(0, tiles)
        def _(i):
            w_copies(i)[1].wait()

        @pl.loop(0, chunks)
        def _(q):
            total = jnp.zeros((rows, hop_width), jnp.float32)
            for i in range(tiles):
                total += jnp.dot(
                    z_keep[0, i], w2[i, :, columns(q)], preferred_element_type=jnp.float32
                )
            acc[:, columns(q)] = total
            f_send[:, columns(q)] = total.astype(jnp.bfloat16)
            start(sum_copies(f_send, f_recv, 0, q))

            @pl.when(q > 0)
            def _():
                pass_on(q - 1)

        pass_on(chunks - 1)

    @pl.loop(0, tiles)
    def _(i):
        z_copy(0, i).start()

    def replica_forward():
        finish(replica_copies(u_all, 0))
        for d in range(1, replicas):

            @pl.loop(0, tiles)
            def _(i):
                activate(d, i)
                z_copy(d, i).start()

        for d in range(replicas):
            flipped = u_all[d, :, kept].astype(jnp.float32).T
            ut[:, d * rows : (d + 1) * rows] = flipped.astype(jnp.bfloat16)
        pltpu.make_async_copy(ut, ut_out, out_sem.at[0, 0]).start()

    @pl.when(jnp.logical_not(last))
    def _():
        replica_forward()
        for q in range(chunks):
            forward_hop(q).wait_send()
        gather(e_all.at[0], 1, backward_hop)
        start(replica_copies(e_all, 1))

        @pl.loop(0, tiles)
        def _(i):
            pregrad(0, i)
            p_copy(0, i).start()

    @pl.loop(0, chunks)
    def _(q):
        total = jnp.zeros((rows, hop_width), jnp.float32)
        for i in range(tiles):
            total += lax.dot_general(
                p_keep[0, i], w1[i, columns(q), :], CONTRACT_LAST, preferred_element_type=jnp.float32
            )
        acc[:, columns(q)] = total

        @pl.when(jnp.logical_not(first))
        def _():
            b_send[:, columns(q)] = total.astype(jnp.bfloat16)
            start(sum_copies(b_send, b_recv, 1, q))

    @pl.when(jnp.logical_not(first))
    def _():
        mine = h_all[my_rows, :].astype(jnp.float32)
        scale = inverse_rms(mine)
        unit = mine * scale
        total = acc[my_rows, :]
        for q in range(chunks):
            finish(sum_copies(b_send, b_recv, 1, q))
        for j in range(1, parts):
            total += b_recv[j].astype(jnp.float32)
        scaled = total * gain_ref[...]
        row_dot = jnp.sum(scaled * unit, axis=1, keepdims=True)
        previous = e_all[0, my_rows, :].astype(jnp.float32) + scale * (
            scaled - unit * (row_dot / full)
        )
        g_hop[...] = previous.astype(jnp.bfloat16)
        for q in range(chunks):
            backward_hop(q).start()

    values = h_all[...].astype(jnp.float32)
    terms = acc[...] * (values * inverse_rms(values))
    gain_part[...] = jnp.sum(terms.reshape(rows // 8, 8, full), axis=0)
    gain_copies = [
        remote(
            gain_part.at[:, pl.ds(pl.multiple_of(part * width, width), width)],
            gain_recv.at[d * parts + j],
            gain_ssem.at[d * parts + j],
            gain_rsem.at[d * parts + j],
            {"dp": other, "mp": part},
        )
        for d, j, other, part in peers
    ]
    start(gain_copies)

    @pl.when(last)
    def _():
        replica_forward()

    finish(replica_copies(e_all, 1))
    for d in range(1, replicas):

        @pl.loop(0, tiles)
        def _(i):
            pregrad(d, i)
            p_copy(d, i).start()

    outs = []
    for d in range(replicas):
        place = pl.ds(d * rows, rows)
        outs.append(pltpu.make_async_copy(e_all.at[d, :, kept], e_out.at[place, :], out_sem.at[1, d]))
    start(outs)
    outs.append(pltpu.make_async_copy(ut, ut_out, out_sem.at[0, 0]))
    total = gain_part[:, my_cols]
    for (d, j, _, _), copy in zip(peers, gain_copies):
        copy.wait()
        total += gain_recv[d * parts + j]
    gain_out[...] = jnp.sum(total, axis=0, keepdims=True)

    for d in range(replicas):

        @pl.loop(0, tiles)
        def _(i):
            z_copy(d, i).wait()
            p_copy(d, i).wait()

    finish(outs)

    @pl.when(jnp.logical_not(first))
    def _():
        for q in range(chunks):
            backward_hop(q).wait_send()


def weight_grads(u_ref, e_ref, p_ref, z_ref, in_ref, out_ref):
    in_ref[...] = jnp.dot(
        u_ref[...], p_ref[...], preferred_element_type=jnp.float32
    ).astype(in_ref.dtype)
    out_ref[...] = lax.dot_general(
        z_ref[...], e_ref[...], CONTRACT_FIRST, preferred_element_type=jnp.float32
    ).astype(out_ref.dtype)


def shards(inputs, cotangent, gain, weight_in, weight_out):
    stages = lax.axis_size("pipe")
    parts = lax.axis_size("mp")
    replicas = lax.axis_size("dp")
    micro, row_count, width = inputs.shape
    rows = micro * row_count
    full = gain.shape[1]
    hidden = weight_in.shape[2]
    tile = math.gcd(hidden, 1024)
    tiles = hidden // tile
    own = rows // parts
    half = full // replicas
    hop_width = math.gcd(full, 256)
    chunks = full // hop_width
    bf16, f32 = jnp.bfloat16, jnp.float32
    vmem = pl.BlockSpec(memory_space=pltpu.VMEM)
    anywhere = pl.BlockSpec(memory_space=pl.ANY)
    dma = pltpu.SemaphoreType.DMA
    z_all, p_all, u_flip, e_cols, gain_total = pl.pallas_call(
        functools.partial(relay, (stages, parts, replicas, hop_width)),
        name="relay",
        out_shape=(
            jax.ShapeDtypeStruct((replicas * rows, hidden), bf16),
            jax.ShapeDtypeStruct((replicas * rows, hidden), bf16),
            jax.ShapeDtypeStruct((half, replicas * rows), bf16),
            jax.ShapeDtypeStruct((replicas * rows, half), bf16),
            jax.ShapeDtypeStruct((1, width), f32),
        ),
        in_specs=[vmem, vmem, vmem, anywhere, anywhere],
        out_specs=(anywhere, anywhere, anywhere, anywhere, vmem),
        scratch_shapes=[
            pltpu.VMEM((tiles, full, tile), bf16),
            pltpu.VMEM((tiles, tile, full), bf16),
            pltpu.VMEM((replicas, tiles, rows, tile), bf16),
            pltpu.VMEM((replicas, tiles, rows, tile), bf16),
            pltpu.VMEM((rows, full), bf16),
            pltpu.VMEM((replicas, rows, full), bf16),
            pltpu.VMEM((half, replicas * rows), bf16),
            pltpu.VMEM((replicas, rows, full), bf16),
            pltpu.VMEM((rows, full), f32),
            pltpu.VMEM((rows, full), bf16),
            pltpu.VMEM((parts, own, full), bf16),
            pltpu.VMEM((rows, full), bf16),
            pltpu.VMEM((parts, own, full), bf16),
            pltpu.VMEM((own, full), bf16),
            pltpu.VMEM((own, full), bf16),
            pltpu.VMEM((8, full), f32),
            pltpu.VMEM((replicas * parts, 8, width), f32),
            dma((tiles,)),
            dma((tiles,)),
            dma((replicas, tiles)),
            dma((replicas, tiles)),
            dma((2, replicas)),
            dma((parts,)),
            dma((parts,)),
            dma((4, chunks)),
            dma((2, chunks, parts)),
            dma((2, chunks, parts)),
            dma((2, replicas)),
            dma((2, replicas)),
            dma((2, chunks, parts)),
            dma((2, chunks, parts)),
            dma((replicas * parts,)),
            dma((replicas * parts,)),
        ],
        compiler_params=pltpu.CompilerParams(
            collective_id=0, has_side_effects=True, vmem_limit_bytes=67043328
        ),
    )(
        inputs.reshape(rows, width),
        cotangent.reshape(rows, width),
        gain,
        weight_in[0],
        weight_out[0],
    )
    count = replicas * rows
    grad_first, grad_second = pl.pallas_call(
        weight_grads,
        name="weight_grads",
        grid=(tiles,),
        out_shape=(
            jax.ShapeDtypeStruct((full // replicas, hidden), bf16),
            jax.ShapeDtypeStruct((hidden, half), bf16),
        ),
        in_specs=[
            vmem,
            vmem,
            pl.BlockSpec((count, tile), lambda i: (0, i)),
            pl.BlockSpec((count, tile), lambda i: (0, i)),
        ],
        out_specs=(
            pl.BlockSpec((half, tile), lambda i: (0, i)),
            pl.BlockSpec((tile, half), lambda i: (i, 0)),
        ),
        compiler_params=pltpu.CompilerParams(vmem_limit_bytes=67043328),
    )(u_flip, e_cols, p_all, z_all)
    return (grad_first[None], grad_second[None], gain_total)


def solution(mesh):
    in_specs = (
        P(None, "dp", "mp"),
        P(None, "dp", "mp"),
        P("pipe", None),
        P("pipe", None, "mp"),
        P("pipe", "mp", None),
    )
    out_specs = (P("pipe", "dp", "mp"), P("pipe", "mp", "dp"), P("pipe", "mp"))
    return jax.shard_map(shards, mesh=mesh, in_specs=in_specs, out_specs=out_specs, check_vma=False)
```
